32 devices in a mesh: param: 4 (over x, core), space: 8 (over z, y).
Axes of the slice: x: 2, y: 2, z: 4, core: 2. Of those that a mesh axis runs over, the one named last changes fastest.
Arguments:
- fine_state: bfloat16 [16, 16, 64, 512], P('space', None, None, 'param'), may hold values from -6 to 6
- fine_tangent: bfloat16 [16, 16, 64, 512], P('space', None, None, 'param'), may hold values from -6 to 6
- down_weight: float32 [8, 512, 1024], P(None, 'space', 'param'), may hold values from -0.09375 to 0.09375
- conv_weight: float32 [27, 1024, 1024], P(None, 'space', 'param'), may hold values from -0.0390625 to 0.0390625
- up_weight: float32 [8, 1024, 512], P(None, 'space', 'param'), may hold values from -0.1875 to 0.1875
Outputs:
- state_out: bfloat16 [16, 16, 64, 512], P('space', None, None, 'param')
- tangent_out: bfloat16 [16, 16, 64, 512], P('space', None, None, 'param')
The draws below stay inside these ranges and needn't reach their ends.
All inputs are finite; a program needn't handle non-finite values.
Results may differ from the reference program's by a relative error of at most 0.0075.
Values may be sent and summed in bfloat16 or wider, within the bound.
No kernel may reach another device: no remote copies, remote signals or barrier semaphores. Data moves between devices by JAX's collectives and lax.ppermute only.
A program may use at most 128 MiB of HBM per device.

```python
import jax
import jax.numpy as jnp

CF = 512
CC = 1024
CY = 8
CX = 32
CZ = 8
FZ = 16
FY = 16
FX = 64


def block_scale(key, extent, shards, least, high):
    gain = 1.0
    for axis_at, shards_of in shards:
        heights = jax.random.uniform(jax.random.fold_in(jax.random.fold_in(key, 6), axis_at), (shards_of,), jnp.float32, least / len(shards), high / len(shards))
        gain = gain * jnp.repeat(jnp.exp(heights), extent[axis_at] // shards_of).reshape((-1,) + (1,) * (len(extent) - 1 - axis_at))
    return gain


def noise(key, shape, spread, reach, shards=(), dtype=jnp.bfloat16):
    array = spread * jax.random.normal(key, shape, jnp.float32)
    if shards:
        array = array * block_scale(key, shape, shards, -0.22, 0.18)
    return jnp.clip(array, -reach, reach).astype(dtype)


def setup_inputs(seed: int = 0) -> dict:
    arg_keys = jax.random.split(jax.random.key(seed), 6)
    return {
        "fine_state": noise(arg_keys[0], (FZ, FY, FX, CF), 1.0, 6.0, ((0, 8), (3, 4))),
        "fine_tangent": noise(arg_keys[1], (FZ, FY, FX, CF), 1.0, 6.0, ((0, 8), (3, 4))),
        "down_weight": noise(arg_keys[2], (8, CF, CC), (8 * CF) ** -0.5, 0.09375, ((1, 8), (2, 4)), jnp.float32),
        "conv_weight": noise(arg_keys[3], (27, CC, CC), (27 * CC) ** -0.5, 0.0390625, ((1, 8), (2, 4)), jnp.float32),
        "up_weight": noise(arg_keys[4], (8, CC, CF), CC ** -0.5, 0.1875, ((1, 8), (2, 4)), jnp.float32),
    }


def silu_pair(primal, tangent):
    sigma = jax.nn.sigmoid(primal)
    return primal * sigma, sigma * (1.0 + primal * (1.0 - sigma)) * tangent


def strided_down(field, kernel):
    patches = field.reshape(CZ, 2, CY, 2, CX, 2, CF).transpose(0, 2, 4, 1, 3, 5, 6).reshape(CZ * CY * CX, 8 * CF)
    return jnp.dot(patches, kernel.reshape(8 * CF, CC), preferred_element_type=jnp.float32)


def cube_conv(field, kernel):
    padded = jnp.pad(field.reshape(CZ, CY, CX, CC), ((1, 1), (1, 1), (1, 1), (0, 0)))
    result = jnp.zeros((CZ * CY * CX, CC), jnp.float32)
    for tap_z in range(3):
        for tap_y in range(3):
            for tap_x in range(3):
                window = padded[tap_z:tap_z + CZ, tap_y:tap_y + CY, tap_x:tap_x + CX, :].reshape(CZ * CY * CX, CC)
                result = result + jnp.dot(window, kernel[9 * tap_z + 3 * tap_y + tap_x], preferred_element_type=jnp.float32)
    return result


def strided_up(field, kernel):
    product = jnp.dot(field, kernel.transpose(1, 0, 2).reshape(CC, 8 * CF), preferred_element_type=jnp.float32)
    return product.reshape(CZ, CY, CX, 2, 2, 2, CF).transpose(0, 3, 1, 4, 2, 5, 6).reshape(2 * CZ, 2 * CY, 2 * CX, CF)


def reference(fine_state, fine_tangent, down_weight, conv_weight, up_weight):
    down_kernel = down_weight.astype(jnp.bfloat16)
    cube_kernel = conv_weight.astype(jnp.bfloat16)
    up_kernel = up_weight.astype(jnp.bfloat16)
    first_pre = strided_down(fine_state, down_kernel)
    first_tan = strided_down(fine_tangent, down_kernel)
    first_val, first_dir = silu_pair(first_pre, first_tan)
    first_val = first_val.astype(jnp.bfloat16)
    first_dir = first_dir.astype(jnp.bfloat16)
    second_pre = cube_conv(first_val, cube_kernel)
    second_tan = cube_conv(first_dir, cube_kernel)
    second_val, second_dir = silu_pair(second_pre, second_tan)
    second_val = (second_val + first_val.astype(jnp.float32)).astype(jnp.bfloat16)
    second_dir = (second_dir + first_dir.astype(jnp.float32)).astype(jnp.bfloat16)
    state_out = strided_up(second_val, up_kernel).astype(jnp.bfloat16)
    tangent_out = strided_up(second_dir, up_kernel).astype(jnp.bfloat16)
    return (state_out, tangent_out)
```

```python
import functools

import jax
import jax.numpy as jnp
from jax import lax
from jax.experimental import pallas as pl
from jax.experimental.pallas import tpu as pltpu
from jax.sharding import PartitionSpec as P

BF16 = jnp.bfloat16
F32 = jnp.float32
VMEM = pl.BlockSpec(memory_space=pltpu.VMEM)
SMEM = pl.BlockSpec(memory_space=pltpu.SMEM)


def silu_pair(primal, tangent):
    sigma = jax.nn.sigmoid(primal)
    return (primal * sigma, sigma * (1.0 + primal * (1.0 - sigma)) * tangent)


def call(kernel, out_shape, args, scratch=(), flops=0, scalars=1):
    outs = jax.tree.leaves(out_shape)
    moved = sum(a.size * a.dtype.itemsize for a in (*args, *outs))
    return pl.pallas_call(
        kernel,
        out_shape=out_shape,
        in_specs=[SMEM] * scalars + [VMEM] * (len(args) - scalars),
        out_specs=jax.tree.map(lambda _: VMEM, out_shape),
        scratch_shapes=list(scratch),
        cost_estimate=pl.CostEstimate(flops=flops, bytes_accessed=moved, transcendentals=0),
        compiler_params=pltpu.CompilerParams(vmem_limit_bytes=60 * 1024 * 1024),
    )(*args)


def xor_permute(block, axis, mask):
    count = lax.axis_size(axis)
    return lax.ppermute(block, axis, [(i, i ^ mask) for i in range(count)])


def shift_permute(block, axis, step):
    count = lax.axis_size(axis)
    return lax.ppermute(block, axis, [(i, (i + step) % count) for i in range(count)])


def gather_space(shard):
    deep = lax.axis_size("space") // 2
    column = [(0, shard)]
    up = down = shard
    for step in range(1, deep // 2 + 1):
        up = shift_permute(up, "space", 2)
        column.append((-step % deep, up))
        if 2 * step < deep:
            down = shift_permute(down, "space", -2)
            column.append((step, down))
    across = [(far, xor_permute(block, "space", 1)) for far, block in column]
    return column, across


def gather_param(blocks):
    held = [blocks]
    mask = lax.axis_size("param") // 2
    masks = [0]
    while mask:
        held += [[xor_permute(b, "param", mask) for b in group] for group in held]
        masks += [m ^ mask for m in masks]
        mask //= 2
    return [held[masks.index(d)] for d in range(len(masks))]


def patch_kernel(state_ref, tangent_ref, out_ref, wide):
    span_y, span_x = state_ref.shape[1] // 2, state_ref.shape[2] // 2
    cells = span_y * span_x
    for at, ref in enumerate((state_ref, tangent_ref)):
        for dz in range(2):
            wide[...] = ref[dz].astype(F32)
            for dy in range(2):
                for dx in range(2):
                    tap = 4 * dz + 2 * dy + dx
                    for y in range(span_y):
                        row = at * cells + y * span_x
                        out_ref[tap, row : row + span_x, :] = wide[
                            2 * y + dy, pl.ds(dx, span_x, stride=2), :
                        ].astype(BF16)


def make_down(acts, column, across):
    n_act, n_col = len(acts), len(column)
    taps, rows, depth = acts[0].shape
    _, part, width = column[0][1].shape
    parts = depth // part
    deep = n_col
    half = width // 2

    def kernel(ids_ref, *refs):
        act_refs = refs[:n_act]
        shard_refs = refs[n_act : n_act + 2 * n_col]
        first_ref, same_ref, cross_ref, weight = refs[n_act + 2 * n_col :]
        p, s = ids_ref[0], ids_ref[1]
        z, y = s // 2, s % 2
        for k, (far, _) in enumerate(column):
            owner = 2 * ((z + far) % deep)
            weight[owner + y] = shard_refs[k][...]
            weight[owner + 1 - y] = shard_refs[n_col + k][...]
        total = None
        for d in range(n_act):
            group = (p ^ d) * parts
            left = jnp.concatenate([act_refs[d][t] for t in range(taps)], axis=1)
            right = jnp.concatenate(
                [weight[group + b, t] for t in range(taps) for b in range(parts)], axis=0
            )
            term = jnp.dot(left, right, preferred_element_type=F32)
            total = term if total is None else total + term
        cells = rows // 2
        value, slope = silu_pair(total[:cells], total[cells:])
        first = jnp.concatenate([value, slope], axis=0).astype(BF16)
        first_ref[...] = first
        low, high = first[:, :half], first[:, half:]
        same_ref[...] = jnp.where(y == 0, low, high)
        cross_ref[...] = jnp.where(y == 0, high, low)

    def run(ids):
        out = (
            jax.ShapeDtypeStruct((rows, width), BF16),
            jax.ShapeDtypeStruct((rows, half), BF16),
            jax.ShapeDtypeStruct((rows, half), BF16),
        )
        return call(
            kernel,
            out,
            (ids, *acts, *[b for _, b in column], *[b for _, b in across]),
            scratch=[pltpu.VMEM((2 * deep, taps, part, width), BF16)],
            flops=2 * rows * taps * depth * n_act * width,
        )

    return run


def make_window(pieces, span_y, span_x):
    flat = [b for pair in pieces for b in pair]
    rows, depth = flat[0].shape
    cells = rows // 2
    planes = len(flat)
    tall = cells + 2 * span_x

    def kernel(ids_ref, *refs):
        out_ref = refs[-1]
        p, y = ids_ref[0], ids_ref[1] % 2
        edge = jnp.zeros((2, tall, 3 * depth), BF16)
        out_ref[:, 0] = edge
        out_ref[:, planes + 1] = edge
        lane_x = lax.broadcasted_iota(jnp.int32, (cells, depth), 0) % span_x
        rim = jnp.zeros((span_x, 3 * depth), BF16)
        for d in range(len(pieces)):
            for i in range(2):
                plane = 2 * (p ^ d) + (y if i == 0 else 1 - y) + 1
                for t in range(2):
                    here = refs[2 * d + i][t * cells : (t + 1) * cells, :]
                    wide = here.astype(F32)
                    left = jnp.where(lane_x == 0, 0.0, pltpu.roll(wide, 1, 0))
                    right = jnp.where(lane_x == span_x - 1, 0.0, pltpu.roll(wide, cells - 1, 0))
                    out_ref[t, plane, :span_x, :] = rim
                    out_ref[t, plane, span_x + cells :, :] = rim
                    body = jnp.concatenate([left.astype(BF16), here, right.astype(BF16)], axis=1)
                    out_ref[t, plane, span_x : span_x + cells, :] = body

    def run(ids):
        out = jax.ShapeDtypeStruct((2, planes + 2, tall, 3 * depth), BF16)
        return call(kernel, out, (ids, *flat))

    return run


def cube_planes(ids, windows, weights, span_x, own, dtype):
    _, tall_z, tall, deep = windows.shape
    cells = tall - 2 * span_x
    width = weights.shape[1]
    count = (tall_z - 2) // 2

    def kernel(ids_ref, win_ref, weight_ref, *out_refs):
        s = ids_ref[1]
        z = s // 2
        parity = s % 2 if own else 1 - s % 2
        for e in range(count):
            plane = 2 * (z ^ e) + parity
            left = jnp.concatenate(
                [
                    jnp.concatenate(
                        [
                            win_ref[t, plane + kz, ky * span_x : ky * span_x + cells, :]
                            for kz in range(3)
                            for ky in range(3)
                        ],
                        axis=1,
                    )
                    for t in range(2)
                ],
                axis=0,
            )
            out_refs[e][...] = jnp.dot(
                left, weight_ref[...], preferred_element_type=F32
            ).astype(dtype)

    out = tuple(jax.ShapeDtypeStruct((2 * cells, width), dtype) for _ in range(count))
    return call(
        kernel, out, (ids, windows, weights), flops=2 * count * 2 * cells * width * 9 * deep
    )


def make_up(acts, column, across, span_y, span_x):
    n_act, n_col = len(acts), len(column)
    rows, depth = acts[0].shape
    taps, part, width = column[0][1].shape
    parts = depth // part
    deep = n_col
    cells = rows // 2

    def kernel(ids_ref, *refs):
        act_refs = refs[:n_act]
        shard_refs = refs[n_act : n_act + 2 * n_col]
        state_ref, tangent_ref, weight, wide = refs[n_act + 2 * n_col :]
        p, s = ids_ref[0], ids_ref[1]
        z, y = s // 2, s % 2
        for k, (far, _) in enumerate(column):
            owner = 2 * ((z + far) % deep)
            weight[owner + y] = shard_refs[k][...]
            weight[owner + 1 - y] = shard_refs[n_col + k][...]
        left = jnp.concatenate([act_refs[d][...] for d in range(n_act)], axis=1)
        for pair in range(taps // 2):
            right = jnp.concatenate(
                [
                    jnp.concatenate(
                        [weight[(p ^ d) * parts + b, 2 * pair + dx] for dx in range(2)], axis=1
                    )
                    for d in range(n_act)
                    for b in range(parts)
                ],
                axis=0,
            )
            product = jnp.dot(left, right, preferred_element_type=F32)
            dz, dy = pair // 2, pair % 2
            for at, ref in enumerate((state_ref, tangent_ref)):
                for row in range(span_y):
                    base = at * cells + row * span_x
                    for dx in range(2):
                        wide[row, pl.ds(dx, span_x, stride=2), :] = product[
                            base : base + span_x, dx * width : (dx + 1) * width
                        ]
                for row in range(span_y):
                    ref[dz, 2 * row + dy] = wide[row].astype(BF16)

    def run(ids):
        out = jax.ShapeDtypeStruct((2, 2 * span_y, 2 * span_x, width), BF16)
        return call(
            kernel,
            (out, out),
            (ids, *acts, *[b for _, b in column], *[b for _, b in across]),
            scratch=[
                pltpu.VMEM((2 * deep, taps, part, width), BF16),
                pltpu.VMEM((span_y, 2 * span_x, width), F32),
            ],
            flops=2 * rows * n_act * depth * taps * width,
        )

    return run


def stationary(fine_state, fine_tangent, down_weight, conv_weight, up_weight):
    n_space, n_param = lax.axis_size("space"), lax.axis_size("param")
    span_y, span_x = fine_state.shape[1] // 2, fine_state.shape[2] // 2
    cells = span_y * span_x
    fine_local = fine_state.shape[3]
    p, s = lax.axis_index("param"), lax.axis_index("space")
    ids = jnp.stack([p, s]).astype(jnp.int32)

    down_cols = gather_space(down_weight.astype(BF16))
    patches = call(
        patch_kernel,
        jax.ShapeDtypeStruct((8, 2 * cells, fine_local), BF16),
        (fine_state, fine_tangent),
        scratch=[pltpu.VMEM((2 * span_y, 2 * span_x, fine_local), F32)],
        scalars=0,
    )
    acts = [group[0] for group in gather_param([patches])]
    first, same, cross = make_down(acts, *down_cols)(ids)

    def transpose(block, flip):
        route = []
        for source in range(n_param * n_space):
            own_p, own_s = divmod(source, n_space)
            z, y = divmod(own_s, 2)
            route.append((source, z * n_space + 2 * own_p + (y ^ flip)))
        return lax.ppermute(block, ("param", "space"), route)

    pieces = gather_param([transpose(same, 0), transpose(cross, 1)])
    windows = make_window(pieces, span_y, span_x)(ids)
    cube = conv_weight.astype(BF16).reshape(-1, conv_weight.shape[2])
    away = cube_planes(ids, windows, cube, span_x, False, BF16)
    returned = [xor_permute(block, "space", 1) for block in away]
    home = cube_planes(ids, windows, cube, span_x, True, F32)
    sums = [h + r.astype(F32) for h, r in zip(home, returned)]
    total = sums[0]
    for e in range(1, len(sums)):
        total = total + xor_permute(sums[e].astype(BF16), "space", 2 * e).astype(F32)
    value, slope = silu_pair(total[:cells], total[cells:])
    second = (jnp.concatenate([value, slope], axis=0) + first.astype(F32)).astype(BF16)

    up_cols = gather_space(up_weight.astype(BF16))
    tops = [group[0] for group in gather_param([second])]
    return make_up(tops, *up_cols, span_y, span_x)(ids)


def padded(block, sides, width):
    for axis, dim in sides:
        count = lax.axis_size(axis)
        forward = [(i, i + 1) for i in range(count - 1)]
        backward = [(target, source) for source, target in forward]
        low = lax.ppermute(
            lax.slice_in_dim(block, block.shape[dim] - width, None, axis=dim), axis, forward
        )
        high = lax.ppermute(lax.slice_in_dim(block, 0, width, axis=dim), axis, backward)
        block = jnp.concatenate([low, block, high], axis=dim)
    return block


def partner(block, axis, apart):
    count = lax.axis_size(axis)
    route = []
    for low in range(count):
        high = low | 1 << apart
        if high != low and high < count:
            route += [(low, high), (high, low)]
    return lax.ppermute(block, axis, route)


def cube_block(source, kernel, planes):
    span_y = source.shape[2] - 2
    span_x = source.shape[3] - 2
    width = source.shape[4]
    result = None
    for tap_z in range(3):
        for tap_y in range(3):
            window = jnp.stack(
                [
                    source[
                        :, tap_z : tap_z + planes, tap_y : tap_y + span_y, tap_x : tap_x + span_x, :
                    ]
                    for tap_x in range(3)
                ],
                axis=4,
            )
            window = window.reshape(-1, 3 * width)
            first_tap = 9 * tap_z + 3 * tap_y
            weights = kernel[first_tap : first_tap + 3].reshape(3 * width, kernel.shape[2])
            term = jnp.dot(window, weights, preferred_element_type=jnp.float32)
            result = term if result is None else result + term
    return result


def gathered(fine_state, fine_tangent, down_weight, conv_weight, up_weight):
    planes = fine_state.shape[0] // 2
    span_y = fine_state.shape[1] // 2
    span_x = fine_state.shape[2] // 2
    cells = planes * span_y * span_x
    state_full, tangent_full = (
        lax.all_gather(fine_state, "param", axis=3, tiled=True),
        lax.all_gather(fine_tangent, "param", axis=3, tiled=True),
    )
    wide_fine = state_full.shape[3]
    paired = jnp.stack([state_full, tangent_full], axis=0)
    patches = (
        paired.reshape(2, planes, 2, span_y, 2, span_x, 2, wide_fine)
        .transpose(0, 1, 3, 5, 2, 4, 6, 7)
        .reshape(2 * cells, 8, wide_fine)
    )
    down_kernel = down_weight.astype(jnp.bfloat16)
    up_kernel = up_weight.astype(jnp.bfloat16)
    cube_kernel = conv_weight.astype(jnp.bfloat16)
    coarse_local = down_weight.shape[2]
    fine_local = up_weight.shape[2]
    portion = lax.all_gather(down_kernel, "space", axis=1, tiled=True)
    width = portion.shape[1]
    columns = patches.reshape(2 * cells, 8 * width)
    first_pre = jnp.dot(
        columns, portion.reshape(8 * width, portion.shape[2]), preferred_element_type=jnp.float32
    )
    first_pre = first_pre.reshape(2, cells, coarse_local)
    first_val, first_dir = silu_pair(first_pre[0], first_pre[1])
    first_round = jnp.stack(
        [first_val.astype(jnp.bfloat16), first_dir.astype(jnp.bfloat16)], axis=0
    )
    first_stack = first_round.reshape(2, planes, span_y, span_x, coarse_local)
    haloed = padded(first_stack, (("space", 1),), 1)
    every_channel = lax.all_gather(haloed, "param", axis=4, tiled=True)
    position = lax.axis_index("space")
    levels = lax.axis_size("space").bit_length() - 1
    wide_coarse = every_channel.shape[4]
    block_kernel = cube_kernel
    for bit in range(levels - 1):
        partner_block = partner(block_kernel, "space", bit)
        upper = position >> bit & 1
        block_kernel = jnp.where(
            upper == 1,
            jnp.concatenate([partner_block, block_kernel], axis=1),
            jnp.concatenate([block_kernel, partner_block], axis=1),
        )
    half_index = position >> levels - 1
    own_half = lax.dynamic_slice_in_dim(
        every_channel, half_index * (wide_coarse // 2), wide_coarse // 2, 4
    )
    send_half = lax.dynamic_slice_in_dim(
        every_channel, (1 - half_index) * (wide_coarse // 2), wide_coarse // 2, 4
    )
    other_half = partner(send_half, "space", levels - 1)
    own_padded = jnp.pad(own_half, ((0, 0), (0, 0), (1, 1), (1, 1), (0, 0)))
    other_padded = jnp.pad(other_half, ((0, 0), (0, 0), (1, 1), (1, 1), (0, 0)))
    own_sum = cube_block(own_padded, block_kernel, planes)
    other_sum = cube_block(other_padded, block_kernel, planes)
    returned = partner(other_sum.astype(jnp.bfloat16), "space", levels - 1).astype(other_sum.dtype)
    second_pre = (own_sum + returned).reshape(2, cells, coarse_local)
    second_val, second_dir = silu_pair(second_pre[0], second_pre[1])
    second_val = second_val + first_round[0].astype(jnp.float32)
    second_dir = second_dir + first_round[1].astype(jnp.float32)
    top_stack = jnp.stack(
        [second_val.astype(jnp.bfloat16), second_dir.astype(jnp.bfloat16)], axis=0
    )
    top_full = lax.all_gather(top_stack, "param", axis=2, tiled=True)
    top_rows = top_full.reshape(2 * cells, top_full.shape[2])
    portion = lax.all_gather(up_kernel, "space", axis=1, tiled=True)
    width = portion.shape[1]
    columns = top_rows
    product = jnp.dot(
        columns,
        portion.transpose(1, 0, 2).reshape(width, 8 * fine_local),
        preferred_element_type=jnp.float32,
    )
    shaped = product.reshape(2, planes, span_y, span_x, 2, 2, 2, fine_local).transpose(
        0, 1, 4, 2, 5, 3, 6, 7
    )
    outputs = shaped.reshape(2, 2 * planes, 2 * span_y, 2 * span_x, fine_local).astype(jnp.bfloat16)
    return (outputs[0], outputs[1])


def local(fine_state, *weights):
    n_space, n_param = lax.axis_size("space"), lax.axis_size("param")
    if n_space == 2 * n_param and fine_state.shape[0] == 2:
        return stationary(fine_state, *weights)
    return gathered(fine_state, *weights)


def solution(mesh):
    in_specs = (
        P("space", None, None, "param"),
        P("space", None, None, "param"),
        P(None, "space", "param"),
        P(None, "space", "param"),
        P(None, "space", "param"),
    )
    out_specs = (P("space", None, None, "param"), P("space", None, None, "param"))
    return jax.shard_map(local, mesh=mesh, in_specs=in_specs, out_specs=out_specs, check_vma=False)
```
